32 devices in a mesh: dp: 8 (over y, x, core), tensor: 4 (over z).
Axes of the slice: x: 2, y: 2, z: 4, core: 2. Of those that a mesh axis runs over, the one named last changes fastest.
Arguments:
- tokens: bfloat16 [3072, 8192], P('dp', 'tensor'), may hold values from -6 to 6
- w_kv: bfloat16 [8192, 2048], P('tensor'), may hold values from -0.0625 to 0.0625
- a_store: bfloat16 [256, 16, 8192], P('dp', None, 'tensor'), may hold values from -0.0625 to 0.0625
- b_store: bfloat16 [256, 16, 2048], P('dp', None, 'tensor'), may hold values from -1.5 to 1.5
- row_peer: int32 [3072, 1], P('dp'), may hold values from 0 to 7; in each aligned block of 384 rows (0 to 383, 384 to 767, ...) at most 96 rows name the same one
- wanted: int32 [8, 8], replicated, may hold values from 0 to 31
- live_rows: int32 [8], P('dp'), may hold values from 1 to 384, 1536 in all
Outputs:
- kv_out: float32 [3072, 2048], P('dp', 'tensor')
The draws below stay inside these ranges and needn't reach their ends.
Inputs may be any that keep to these rules, and one draw needn't show every extreme that they name: `row_peer`: within one group of 384 rows no owner is named by more than 96 rows, a bound that some block reaches.
All inputs are finite; a program needn't handle non-finite values. No bound on the sum of `live_rows` on one device may be relied on, other than what follows from the above.
Results may differ from the reference program's by a relative error of at most 0.0003.
Values may be sent and summed in bfloat16 or wider, within the bound.
A program may use at most 64 MiB of HBM per device.

```python
import math
import jax
import jax.numpy as jnp
import numpy as np
from jax import lax

D = 8192
KV = 2048
RANK = 16
ADP_DEV = 32
ROWS_DEV = 384
ADAPTERS = 256
ROWS = 3072
ROW_CAP = 96
N_DP = 8
N_TENSOR = 4


def touch_ends(values, own_key, least, high):
    longest = values.shape.index(max(values.shape))
    spots = []
    for shift in (0, 1):
        where = [jax.random.randint(jax.random.fold_in(own_key, axis), (), 0, length) for axis, length in enumerate(values.shape)]
        where[longest] = (where[longest] + shift) % values.shape[longest]
        spots.append(tuple(where))
    return values.at[spots[0]].set(least).at[spots[1]].set(high)


def block_scale(key, extent, pieces, least, top_value):
    loudness, own = 1.0, jax.random.fold_in(key, 6)
    for position, parts in pieces:
        steps = jnp.exp(jax.random.uniform(jax.random.fold_in(own, position), (parts,), jnp.float32, least / len(pieces), top_value / len(pieces)))
        loudness = loudness * jnp.repeat(steps, extent[position] // parts).reshape([-1 if axis == position else 1 for axis in range(len(extent))])
    return loudness


def split_up(count, total, bound, lean):
    weights = [(1 << 20) // math.isqrt(rank ** lean) + 1 for rank in range(2, count + 1)]
    surplus, counts = total - bound - (count - 1), [1] * (count - 1)
    while surplus > 0:
        free = [i for i in range(count - 1) if counts[i] < bound]
        mass, remaining = sum([weights[i] for i in free]), surplus
        for i in free:
            more = min(bound - counts[i], max(1, remaining * weights[i] // mass), surplus)
            counts[i] = counts[i] + more
            surplus = surplus - more
    return np.array([bound] + counts)


def uneven_parts(own_key, count, total, limit, skew):
    if count == 2:
        one = jax.random.randint(own_key, (), max(1, total - limit), min(limit, total - 1) + 1)
        return jnp.stack([one, total - one])
    tallies = jnp.asarray(split_up(count, total, limit, skew), jnp.int32)
    twos = (count - 1) // 2
    donor, taker = tallies[1:1 + 2 * twos:2], tallies[2:2 + 2 * twos:2]
    slack = jnp.minimum(donor - 1, limit - taker)
    moved = jax.random.randint(jax.random.fold_in(own_key, 1), (twos,), 0, 1 << 20) % (slack + 1)
    tallies = tallies.at[1:1 + 2 * twos:2].set(donor - moved).at[2:2 + 2 * twos:2].set(taker + moved)
    return tallies[jax.random.permutation(jax.random.fold_in(own_key, 2), count)]


def routed_block(stream_key, own, number, rows, number_of, top, most, lean):
    ranking = jax.random.permutation(stream_key, number_of)
    crowded, common = shares(number_of, rows * top, most, lean, True), shares(number_of, rows * top, most, lean, False)
    places = jnp.arange(number_of)

    def named(sizes, rotation):
        used = int((sizes > 0).sum())
        fixed = max(1, used // 4)
        passed = fixed + (places - fixed + rotation * (used - fixed)) % max(1, number_of - fixed)
        return jnp.zeros((number_of,), jnp.int32).at[ranking[jnp.where(places < fixed, places, passed)]].set(jnp.asarray(sizes, jnp.int32))

    sizes = jnp.where(number % 4 == 0, named(crowded, number // 4), named(common, number - number // 4 - 1))
    mixed = jax.random.permutation(jax.random.fold_in(own, 3), number_of)
    giver, receiver = mixed[0:number_of // 2 * 2:2], mixed[1:number_of // 2 * 2:2]
    margin = jnp.minimum(sizes[giver] - 1, most - sizes[receiver]) // 2
    margin = jnp.where((giver == ranking[0]) | (receiver == ranking[0]) | (sizes[receiver] == 0), 0, jnp.maximum(margin, 0))
    passed = jax.random.randint(jax.random.fold_in(own, 4), (number_of // 2,), 0, 1 << 20) % (margin + 1)
    sizes = sizes.at[giver].add(-passed).at[receiver].add(passed)
    items = jnp.searchsorted(jnp.cumsum(sizes), jnp.arange(rows * top), side="right").astype(jnp.int32)
    grid = items.reshape(top, rows).T
    grid = grid[jax.random.permutation(jax.random.fold_in(own, 1), rows)]
    rotation = jax.random.randint(jax.random.fold_in(own, 2), (rows, 1), 0, top)
    return jnp.take_along_axis(grid, (jnp.arange(top)[None, :] + rotation) % top, axis=1)


def shares(number_of, total, reach, lean, full):
    portions = [(1 << 20) // math.isqrt(standing ** lean) + 1 for standing in range(1, number_of + 1)]
    largest = reach if full else min(reach, max(-(-total // number_of), total * portions[0] // sum(portions)))
    least = 1 if total - largest >= number_of - 1 else 0
    counts, spare = [largest] + [least] * (number_of - 1), total - largest - least * (number_of - 1)
    while spare > 0:
        candidates = [i for i in range(1, number_of) if counts[i] < largest] or [i for i in range(1, number_of) if counts[i] < reach]
        whole, budget = sum([portions[i] for i in candidates]), spare
        for i in candidates:
            extra = min(reach - counts[i], max(1, budget * portions[i] // whole), spare)
            counts[i] = counts[i] + extra
            spare = spare - extra
    return np.array(counts)


def normal_values(key, dims, deviation, reach, split=(), kind=jnp.bfloat16):
    entries = deviation * jax.random.normal(key, dims, jnp.float32)
    if split:
        entries = entries * block_scale(key, dims, split, -0.22, 0.18)
    return jnp.clip(entries, -reach, reach).astype(kind)


def setup_inputs(seed: int = 0) -> dict:
    keys = jax.random.split(jax.random.key(seed), 8)
    tokens = normal_values(keys[0], (ROWS, D), 1.0, 6.0, ((0, 8), (1, 4)))
    w_kv = normal_values(keys[1], (D, KV), D ** -0.5, 0.0625, ((0, 4),))
    a_store = normal_values(keys[2], (ADAPTERS, RANK, D), D ** -0.5, 0.0625, ((0, 8), (2, 4)))
    b_store = normal_values(keys[3], (ADAPTERS, RANK, KV), RANK ** -0.5, 1.5, ((0, 8), (2, 4)))
    row_peer_keys = jax.random.split(jax.random.fold_in(keys[4], 1), ROWS // ROWS_DEV)
    row_peer_turns = jax.random.permutation(jax.random.fold_in(keys[4], 3), ROWS // ROWS_DEV)
    row_peer = jax.vmap(lambda own, number: routed_block(jax.random.fold_in(keys[4], 2), own, number, ROWS_DEV, N_DP, 1, ROW_CAP, 2))(row_peer_keys, row_peer_turns).reshape((ROWS, 1))
    wanted = touch_ends(jax.random.randint(keys[5], (N_DP, N_DP), 0, ADP_DEV), jax.random.fold_in(keys[5], 1), 0, ADP_DEV - 1).astype(jnp.int32)
    live_rows = uneven_parts(keys[6], N_DP, N_DP * ROWS_DEV // 2, ROWS_DEV, 2).astype(jnp.int32)
    return dict(tokens=tokens, w_kv=w_kv, a_store=a_store, b_store=b_store, row_peer=row_peer, wanted=wanted, live_rows=live_rows)


def reference(tokens, w_kv, a_store, b_store, row_peer, wanted, live_rows):
    width = D // N_TENSOR

    def add_block(carry, block):
        start = (block * width).astype(jnp.int32)
        xs = lax.dynamic_slice_in_dim(tokens, start, width, 1)
        ws = lax.dynamic_slice_in_dim(w_kv, start, width, 0)
        part = jnp.dot(xs, ws, preferred_element_type=jnp.float32)
        return carry + part, None

    base, _ = lax.scan(add_block, jnp.zeros((ROWS, KV), jnp.float32), jnp.arange(N_TENSOR, dtype=jnp.int32))
    peers = row_peer[:, 0].astype(jnp.int32)
    groups = (jnp.arange(ROWS, dtype=jnp.int32) // ROWS_DEV).astype(jnp.int32)
    slot = (peers * ADP_DEV + wanted[groups, peers]).astype(jnp.int32)

    def one_group(args):
        rows_x, rows_slot = args
        a_rows = a_store[rows_slot].astype(jnp.float32)
        shrink = jnp.einsum("rf,rkf->rk", rows_x.astype(jnp.float32), a_rows, precision=lax.Precision.HIGHEST)
        b_rows = b_store[rows_slot].astype(jnp.float32)
        return jnp.einsum("rk,rkc->rc", shrink, b_rows, precision=lax.Precision.HIGHEST)

    delta = lax.map(one_group, (tokens.reshape(N_DP, ROWS_DEV, D), slot.reshape(N_DP, ROWS_DEV)))
    delta = delta.reshape(ROWS, KV)
    inside = (jnp.arange(ROWS, dtype=jnp.int32) % ROWS_DEV) < live_rows[groups]
    return jnp.where(inside[:, None], base + delta, 0.0).astype(jnp.float32)
```

```python
import functools
import jax
import jax.numpy as jnp
from jax import lax
from jax.experimental import pallas as pl
from jax.experimental.pallas import tpu as pltpu
from jax.sharding import PartitionSpec as P

MESH = pl.DeviceIdType.MESH
LINK = jnp.int16
STEPS = 32766.0
LEAST = 1e-30
CHUNKS = 2
LAG = 1


def encode(x):
    top = jnp.maximum(jnp.max(jnp.abs(x), axis=0, keepdims=True), LEAST)
    code = jnp.round(x * (STEPS / top)).astype(jnp.int32).astype(LINK)
    return code, top * (1.0 / STEPS)


def decode(code, step):
    return code.astype(jnp.int32).astype(jnp.float32) * step


def kernel(n, owners, wanted, live, tok_hbm, w_hbm, a_hbm, b_hbm, peer_ref, out_ref,
           tok, w, a_vm, b_vm, part, zs, zr, us, ur, a_out, a_in, b_out, b_in, s_out, s_in,
           tok_sem, w_sem, a_sem, b_sem, zs_sem, zr_sem, us_sem, ur_sem, as_sem, ar_sem, bs_sem, br_sem,
           ss_sem, sr_sem):
    p = lax.axis_index("tensor")
    me = lax.axis_index("dp")
    rows = tok.shape[0]
    blk = w.shape[2]
    rank = a_vm.shape[1]
    ch = zs.shape[2]
    rc = rows // ch

    def w_copy(d):
        cols = pl.ds(pl.multiple_of(d * blk, blk), blk)
        return pltpu.make_async_copy(w_hbm.at[:, cols], w.at[d], w_sem.at[d])

    def place(t):
        s = t // 2
        way = t % 2
        d = jnp.where(way == 0, n - 1 - s, s)
        return s, way, d

    def ahead(way, d):
        return ((way == 0) & (d > p)) | ((way == 1) & (d < p))

    def first_hop(way):
        return ((way == 0) & (p == 0)) | ((way == 1) & (p == n - 1))

    def z_copy(way, s, c, q):
        return pltpu.make_async_remote_copy(
            src_ref=zs.at[way, s, c], dst_ref=zr.at[way, s, c],
            send_sem=zs_sem.at[way, s, c], recv_sem=zr_sem.at[way, s, c],
            device_id={"tensor": q}, device_id_type=MESH)

    def u_copy(way, s, c, q):
        return pltpu.make_async_remote_copy(
            src_ref=us.at[way, s, c], dst_ref=ur.at[way, s, c],
            send_sem=us_sem.at[way, s, c], recv_sem=ur_sem.at[way, s, c],
            device_id={"tensor": q}, device_id_type=MESH)

    def put(way, s, c, q, value):
        code, step = encode(value)
        us[way, s, c] = step
        zs[way, s, c] = code
        u_copy(way, s, c, q).start()
        z_copy(way, s, c, q).start()

    def get(way, s, c, q):
        u_copy(way, s, c, q).wait_recv()
        z_copy(way, s, c, q).wait_recv()
        return decode(zr[way, s, c], ur[way, s, c])

    def a_copy(j, slot):
        return pltpu.make_async_remote_copy(
            src_ref=a_out.at[j], dst_ref=a_in.at[slot],
            send_sem=as_sem.at[j], recv_sem=ar_sem.at[slot],
            device_id={"dp": j}, device_id_type=MESH)

    def b_copy(j, slot):
        return pltpu.make_async_remote_copy(
            src_ref=b_out.at[j], dst_ref=b_in.at[slot],
            send_sem=bs_sem.at[j], recv_sem=br_sem.at[slot],
            device_id={"dp": j}, device_id_type=MESH)

    def s_copy(q, slot):
        return pltpu.make_async_remote_copy(
            src_ref=s_out, dst_ref=s_in.at[slot],
            send_sem=ss_sem.at[q], recv_sem=sr_sem.at[slot],
            device_id={"tensor": q}, device_id_type=MESH)

    barrier = pltpu.get_barrier_semaphore()

    @pl.loop(1, owners)
    def _(k):
        pl.semaphore_signal(barrier, inc=1, device_id={"dp": lax.rem(me + k, owners)},
                            device_id_type=MESH)

    @pl.loop(1, n)
    def _(k):
        pl.semaphore_signal(barrier, inc=1, device_id={"tensor": lax.rem(p + k, n)},
                            device_id_type=MESH)

    tok_copy = pltpu.make_async_copy(tok_hbm, tok, tok_sem)
    tok_copy.start()

    def load(t):
        s, way, d = place(t)

        @pl.when(ahead(way, d))
        def _():
            w_copy(d).start()

    pl.loop(0, 2)(load)
    a_load = pltpu.make_async_copy(a_hbm, a_vm, a_sem)
    b_load = pltpu.make_async_copy(b_hbm, b_vm, b_sem)
    tok_copy.wait()

    def multiply(d, c):
        span = pl.ds(pl.multiple_of(c * rc, rc), rc)
        part[d, span] = jnp.dot(tok[span], w[d], preferred_element_type=jnp.float32)

    @pl.loop(0, 2)
    def _(t):
        s, way, d = place(t)

        @pl.when(ahead(way, d))
        def _():
            w_copy(d).wait()

    a_load.start()
    b_load.start()
    pl.loop(2, 2 * (n - 1))(load)
    w_copy(p).start()

    @pl.loop(0, 2)
    def _(t):
        s, way, d = place(t)

        @pl.when(ahead(way, d))
        def _():
            multiply(d, 0)

    pl.semaphore_wait(barrier, owners - 1 + n - 1)

    def fetch():
        a_load.wait()
        b_load.wait()

        @pl.loop(0, owners)
        def _(k):
            j = lax.rem(me + k, owners)
            asked = wanted[j, me]
            a_map = a_vm[asked]
            b_map = b_vm[asked]

            @pl.when(k == 0)
            def _():
                a_in[me] = a_map
                b_in[me] = b_map

            @pl.when(k > 0)
            def _():
                a_out[j] = a_map
                b_out[j] = b_map
                a_copy(j, me).start()
                b_copy(j, me).start()

    def send_first(way, s, d, c):
        q = jnp.where(way == 0, p + 1, p - 1)
        put(way, s, c, q, part[d, pl.ds(pl.multiple_of(c * rc, rc), rc)])

    @pl.loop(0, 2 * (n - 1))
    def _(t):
        s, way, d = place(t)

        @pl.when(ahead(way, d))
        def _():
            @pl.when(t > 1)
            def _():
                w_copy(d).wait()

            @pl.loop(0, ch)
            def _(c):
                @pl.when((t > 1) | (c > 0))
                def _():
                    multiply(d, c)

                @pl.when(first_hop(way) & (s < n - 2))
                def _():
                    send_first(way, s, d, c)

        @pl.when(t == 1)
        def _():
            fetch()

    w_copy(p).wait()
    out_ref[...] = jnp.dot(tok[...], w[p], preferred_element_type=jnp.float32)

    def pass_on(s, c, way):
        d = jnp.where(way == 0, n - 1 - s, s)
        span = pl.ds(pl.multiple_of(c * rc, rc), rc)
        q = jnp.where(way == 0, p + 1, p - 1)
        back = jnp.where(way == 0, p - 1, p + 1)

        @pl.when(jnp.logical_not(first_hop(way)) & ahead(way, d))
        def _():
            put(way, s, c, q, get(way, s, c, back) + part[d, span])

        @pl.when(jnp.logical_not(first_hop(way)) & (d == p))
        def _():
            out_ref[span] += get(way, s, c, back)

    near = jnp.where(2 * p < n - 1, 0, 1)
    lag = LAG * jnp.abs(n - 1 - 2 * p)
    late = LAG * (n - 1)

    def pass_range(low, high):
        @pl.loop(low, high)
        def _(i):
            @pl.when(i < (n - 1) * ch)
            def _():
                pass_on(i // ch, i % ch, near)

            k = i - lag

            @pl.when((k >= 0) & (k < (n - 1) * ch))
            def _():
                pass_on(k // ch, k % ch, 1 - near)

    pass_range(0, ch)

    @pl.loop(1, owners)
    def _(k):
        a_copy(lax.rem(me + k, owners), lax.rem(me + k, owners)).wait()

    width = owners * rank
    named = peer_ref[...]
    mine = lax.broadcasted_iota(jnp.int32, (width, rows), 0) // rank == named
    every = lax.dot_general(a_in[...].reshape(width, a_in.shape[2]), tok[...],
                            (((1,), (1,)), ((), ())), preferred_element_type=jnp.float32)
    kept = jnp.where(mine, every, 0.0).reshape(owners, rank, rows)
    total = kept[0]
    for j in range(1, owners):
        total = total + kept[j]
    s_out[...] = total

    @pl.loop(1, n)
    def _(k):
        q = lax.rem(p + k, n)
        s_copy(q, p).start()

    for way in range(2):
        s = n - 2
        d = n - 1 - s if way == 0 else s

        @pl.when(first_hop(way))
        def _():
            for c in range(ch):
                send_first(way, s, d, c)

    pass_range(ch, (n - 2) * ch)

    @pl.loop(1, owners)
    def _(k):
        b_copy(lax.rem(me + k, owners), lax.rem(me + k, owners)).wait()

    @pl.loop(1, n)
    def _(k):
        q = lax.rem(p + k, n)
        s_copy(q, q).wait()
    total = s_out[...]
    for k in range(1, n):
        total = total + s_in[lax.rem(p + k, n)]
    spread = jnp.broadcast_to(total[None], (owners, rank, rows)).reshape(width, rows)
    shrink = jnp.where(mine, spread, 0.0).T
    high = shrink.astype(jnp.bfloat16)
    low = (shrink - high.astype(jnp.float32)).astype(jnp.bfloat16)
    ups = b_in[...].reshape(width, blk)
    out_ref[...] += (jnp.dot(high, ups, preferred_element_type=jnp.float32)
                     + jnp.dot(low, ups, preferred_element_type=jnp.float32))

    pass_range((n - 2) * ch, (n - 1) * ch + late)
    inside = lax.broadcasted_iota(jnp.int32, (rows, blk), 0) < live[0]
    out_ref[...] = jnp.where(inside, out_ref[...], 0.0)

    @pl.loop(0, 2 * (n - 1))
    def _(t):
        s, way, d = place(t)

        @pl.when(ahead(way, d))
        def _():
            for c in range(ch):
                q = jnp.where(way == 0, p + 1, p - 1)
                u_copy(way, s, c, q).wait_send()
                z_copy(way, s, c, q).wait_send()


def local(n, owners, tokens, w_kv, a_store, b_store, row_peer, wanted, live_rows):
    rows, feat = tokens.shape
    blk = w_kv.shape[1] // n
    held, rank = a_store.shape[:2]
    rc = rows // CHUNKS
    vmem, dma = pltpu.VMEM, pltpu.SemaphoreType.DMA
    anyspec = pl.BlockSpec(memory_space=pl.ANY)
    return pl.pallas_call(
        functools.partial(kernel, n, owners),
        out_shape=jax.ShapeDtypeStruct((rows, blk), jnp.float32),
        in_specs=[pl.BlockSpec(memory_space=pltpu.SMEM), pl.BlockSpec(memory_space=pltpu.SMEM), anyspec, anyspec, anyspec, anyspec,
                  pl.BlockSpec(memory_space=pltpu.VMEM)],
        out_specs=pl.BlockSpec(memory_space=pltpu.VMEM),
        scratch_shapes=[
            vmem((rows, feat), jnp.bfloat16),
            vmem((n, feat, blk), jnp.bfloat16),
            vmem((held, rank, feat), jnp.bfloat16),
            vmem((held, rank, blk), jnp.bfloat16),
            vmem((n, rows, blk), jnp.float32),
            vmem((2, n - 1, CHUNKS, rc, blk), LINK),
            vmem((2, n - 1, CHUNKS, rc, blk), LINK),
            vmem((2, n - 1, CHUNKS, 1, blk), jnp.float32),
            vmem((2, n - 1, CHUNKS, 1, blk), jnp.float32),
            vmem((owners, rank, feat), jnp.bfloat16),
            vmem((owners, rank, feat), jnp.bfloat16),
            vmem((owners, rank, blk), jnp.bfloat16),
            vmem((owners, rank, blk), jnp.bfloat16),
            vmem((rank, rows), jnp.float32),
            vmem((n, rank, rows), jnp.float32),
            dma, dma((n,)), dma, dma,
            dma((2, n - 1, CHUNKS)), dma((2, n - 1, CHUNKS)),
            dma((2, n - 1, CHUNKS)), dma((2, n - 1, CHUNKS)),
            dma((owners,)), dma((owners,)), dma((owners,)), dma((owners,)),
            dma((n,)), dma((n,)),
        ],
        compiler_params=pltpu.CompilerParams(collective_id=0, has_side_effects=True),
        name="project",
    )(wanted, live_rows, tokens, w_kv, a_store, b_store, row_peer.reshape(1, rows))


def solution(mesh):
    in_specs = (
        P("dp", "tensor"),
        P("tensor", None),
        P("dp", None, "tensor"),
        P("dp", None, "tensor"),
        P("dp", None),
        P(),
        P("dp"),
    )
    body = functools.partial(local, mesh.shape["tensor"], mesh.shape["dp"])
    return jax.shard_map(body, mesh=mesh, in_specs=in_specs, out_specs=P("dp", "tensor"),
                         check_vma=False)
```

```python
import functools
import jax
import numpy as np
import jax.numpy as jnp
from jax import lax
from jax.experimental import pallas as pl
from jax.experimental.pallas import tpu as pltpu
from jax.sharding import PartitionSpec as P

MESH = pl.DeviceIdType.MESH
LINK = jnp.int16
STEPS = 32766.0
LEAST = 1e-30
LAG = 1
TILE = 8
SPLIT = 2


def most_pooled(owners, rows, home):
    total = owners * rows // 2
    lengths = np.arange(1, rows + 1)
    best = np.full(total + 1, -1)
    best[0] = 0
    for turn in range(owners):
        got = sum(np.clip(lengths - home - TILE * b, 0, TILE)
                  for b in range(turn, (rows - home) // TILE, owners))
        after = np.full(total + 1, -1)
        for length in range(1, rows + 1):
            before = best[:total + 1 - length]
            after[length:] = np.maximum(after[length:], np.where(before < 0, -1, before + got[length - 1]))
        best = after
    return int(best[total])


def plan(owners, rows):
    home = rows // 2
    cap = home // 2
    if home % (TILE * owners) == 0 and most_pooled(owners, rows, home) <= cap:
        return home, cap, cap // SPLIT
    return rows, 0, rows // 2


def encode(x):
    top = jnp.maximum(jnp.max(jnp.abs(x), axis=0, keepdims=True), LEAST)
    code = jnp.round(x * (STEPS / top)).astype(jnp.int32).astype(LINK)
    return code, top * (1.0 / STEPS)


def decode(code, step):
    return code.astype(jnp.int32).astype(jnp.float32) * step


def kernel(n, owners, home, cap, wanted, live, tok_hbm, w_hbm, a_hbm, b_hbm, peer_ref, out_ref,
           tok, w, a_vm, b_vm, part, zs, zr, us, ur, a_out, a_in, b_out, b_in, s_out, s_in,
           pin, picked, sel, spread_sel, n_out, n_in, r_out, r_in, v_out, v_in,
           tok_sem, w_sem, a_sem, b_sem, zs_sem, zr_sem, us_sem, ur_sem, as_sem, ar_sem, bs_sem, br_sem,
           ss_sem, sr_sem, ts_sem, tr_sem, own_sem, ns_sem, nr_sem, rs_sem, rr_sem, vs_sem, vr_sem):
    p = lax.axis_index("tensor")
    me = lax.axis_index("dp")
    rows = tok.shape[0]
    blk = w.shape[2]
    rank = a_vm.shape[1]
    ch = zs.shape[2]
    rc = zs.shape[3]
    hc = home // rc
    pc = cap // rc
    pool = rows - home
    per = pool // owners
    turns = per // TILE
    edge = (p == 0) | (p == n - 1)

    def w_copy(d):
        cols = pl.ds(pl.multiple_of(d * blk, blk), blk)
        return pltpu.make_async_copy(w_hbm.at[:, cols], w.at[d], w_sem.at[d])

    def place(t):
        s = t // 2
        way = t % 2
        d = jnp.where(way == 0, n - 1 - s, s)
        return s, way, d

    def ahead(way, d):
        return ((way == 0) & (d > p)) | ((way == 1) & (d < p))

    def first_hop(way):
        return ((way == 0) & (p == 0)) | ((way == 1) & (p == n - 1))

    def z_copy(way, s, c, q):
        return pltpu.make_async_remote_copy(
            src_ref=zs.at[way, s, c], dst_ref=zr.at[way, s, c],
            send_sem=zs_sem.at[way, s, c], recv_sem=zr_sem.at[way, s, c],
            device_id={"tensor": q}, device_id_type=MESH)

    def u_copy(way, s, c, q):
        return pltpu.make_async_remote_copy(
            src_ref=us.at[way, s, c], dst_ref=ur.at[way, s, c],
            send_sem=us_sem.at[way, s, c], recv_sem=ur_sem.at[way, s, c],
            device_id={"tensor": q}, device_id_type=MESH)

    def put(way, s, c, q, value):
        code, step = encode(value)
        us[way, s, c] = step
        zs[way, s, c] = code
        u_copy(way, s, c, q).start()
        z_copy(way, s, c, q).start()

    def get(way, s, c, q):
        u_copy(way, s, c, q).wait_recv()
        z_copy(way, s, c, q).wait_recv()
        return decode(zr[way, s, c], ur[way, s, c])

    def dp_copy(src, dst, send, recv, j):
        return pltpu.make_async_remote_copy(
            src_ref=src, dst_ref=dst, send_sem=send, recv_sem=recv,
            device_id={"dp": j}, device_id_type=MESH)

    def a_copy(j, slot):
        return dp_copy(a_out.at[j], a_in.at[slot], as_sem.at[j], ar_sem.at[slot], j)

    def b_copy(j, slot):
        return dp_copy(b_out.at[j], b_in.at[slot], bs_sem.at[j], br_sem.at[slot], j)

    def n_copy(j, slot):
        return dp_copy(n_out, n_in.at[slot], ns_sem.at[j], nr_sem.at[slot], j)

    def r_copy(j, slot):
        return dp_copy(r_out.at[j], r_in.at[slot], rs_sem.at[j], rr_sem.at[slot], j)

    def v_copy(j, slot):
        return dp_copy(v_out, v_in.at[slot], vs_sem.at[j], vr_sem.at[slot], j)

    def source_rows(j, turn):
        b = lax.rem(j - me + owners, owners) + owners * turn
        return tok_hbm.at[pl.ds(pl.multiple_of(home + TILE * b, TILE), TILE), :]

    def slot_rows(slot, turn):
        return pin.at[pl.ds(pl.multiple_of(slot * per + TILE * turn, TILE), TILE), :]

    def t_copy(j, slot, turn):
        return dp_copy(source_rows(j, turn), slot_rows(slot, turn), ts_sem.at[j, turn], tr_sem.at[slot, turn], j)

    def own_copy(turn):
        return pltpu.make_async_copy(source_rows(me, turn), slot_rows(me, turn), own_sem.at[turn])

    def s_copy(q, slot):
        return pltpu.make_async_remote_copy(
            src_ref=s_out, dst_ref=s_in.at[slot],
            send_sem=ss_sem.at[q], recv_sem=sr_sem.at[slot],
            device_id={"tensor": q}, device_id_type=MESH)

    def others(body):
        @pl.loop(1, owners)
        def _(k):
            body(lax.rem(me + k, owners))

    barrier = pltpu.get_barrier_semaphore()

    @pl.loop(1, owners)
    def _(k):
        pl.semaphore_signal(barrier, inc=1, device_id={"dp": lax.rem(me + k, owners)},
                            device_id_type=MESH)

    @pl.loop(1, n)
    def _(k):
        pl.semaphore_signal(barrier, inc=1, device_id={"tensor": lax.rem(p + k, n)},
                            device_id_type=MESH)

    tok_copy = pltpu.make_async_copy(tok_hbm, tok, tok_sem)
    tok_copy.start()

    def load(t):
        s, way, d = place(t)

        @pl.when(ahead(way, d))
        def _():
            w_copy(d).start()

    pl.loop(0, 2 * (n - 1))(load)
    w_copy(p).start()
    a_load = pltpu.make_async_copy(a_hbm, a_vm, a_sem)
    b_load = pltpu.make_async_copy(b_hbm, b_vm, b_sem)
    a_load.start()
    b_load.start()

    if pool:
        n_out[...] = jnp.full(n_out.shape, live[0], jnp.int32)
        for turn in range(turns):
            own_copy(turn).start()

    pl.semaphore_wait(barrier, owners - 1 + n - 1)

    if pool:
        def scatter(j):
            n_copy(j, me).start()
            for turn in range(turns):
                t_copy(j, me, turn).start()

        others(scatter)
        n_in[me] = n_out[...]

    tok_copy.wait()

    def send_first(way, s, d, c):
        q = jnp.where(way == 0, p + 1, p - 1)
        put(way, s, c, q, part[d, pl.ds(pl.multiple_of(c * rc, rc), rc)])

    @pl.loop(0, 2 * (n - 1))
    def _(t):
        s, way, d = place(t)

        @pl.when(ahead(way, d))
        def _():
            w_copy(d).wait()

            @pl.loop(0, SPLIT)
            def _(h):
                span = pl.ds(pl.multiple_of(h * (home // SPLIT), home // SPLIT), home // SPLIT)
                part[d, span] = jnp.dot(tok[span], w[d], preferred_element_type=jnp.float32)

                @pl.when(first_hop(way) & (s < n - 2))
                def _():
                    @pl.loop(0, hc // SPLIT)
                    def _(c):
                        send_first(way, s, d, h * (hc // SPLIT) + c)

    a_load.wait()
    b_load.wait()

    @pl.loop(0, owners)
    def _(k):
        j = lax.rem(me + k, owners)
        asked = wanted[j, me]
        a_map = a_vm[asked]
        b_map = b_vm[asked]

        @pl.when(k == 0)
        def _():
            a_in[me] = a_map
            b_in[me] = b_map

        @pl.when(k > 0)
        def _():
            a_out[j] = a_map
            b_out[j] = b_map
            a_copy(j, me).start()
            b_copy(j, me).start()

    w_copy(p).wait()
    part[p, pl.ds(0, home)] = jnp.dot(tok[pl.ds(0, home)], w[p], preferred_element_type=jnp.float32)

    def pass_on(s, c, way):
        d = jnp.where(way == 0, n - 1 - s, s)
        span = pl.ds(pl.multiple_of(c * rc, rc), rc)
        q = jnp.where(way == 0, p + 1, p - 1)
        back = jnp.where(way == 0, p - 1, p + 1)

        @pl.when(jnp.logical_not(first_hop(way)) & ahead(way, d))
        def _():
            put(way, s, c, q, get(way, s, c, back) + part[d, span])

        @pl.when(jnp.logical_not(first_hop(way)) & (d == p))
        def _():
            part[p, span] += get(way, s, c, back)

    near = jnp.where(2 * p < n - 1, 0, 1)
    lag = LAG * jnp.abs(n - 1 - 2 * p)
    late = LAG * (n - 1)
    early = (n - 2) * hc
    mid = (n - 1) * pc
    count = (n - 1) * ch
    done = early + max(mid, pc + late)

    def item(i):
        if not pool:
            return lax.div(i, hc), lax.rem(i, hc)
        k = i - early
        m = k - mid
        s = jnp.where(k < 0, lax.div(i, hc), jnp.where(m < 0, lax.div(k, pc), n - 2))
        c = jnp.where(k < 0, lax.rem(i, hc), jnp.where(m < 0, hc + lax.rem(k, pc), m))
        return s, c

    def pass_range(low, high):
        @pl.loop(low, high)
        def _(i):
            @pl.when(i < count)
            def _():
                s, c = item(i)
                pass_on(s, c, near)

            k = i - lag

            @pl.when((k >= 0) & (k < count))
            def _():
                s, c = item(k)
                pass_on(s, c, 1 - near)

    pass_range(0, early)

    def last_home(low, high):
        for way in range(2):
            s = n - 2
            d = n - 1 - s if way == 0 else s

            @pl.when(first_hop(way))
            def _():
                @pl.loop(low, high)
                def _(c):
                    send_first(way, s, d, c)

    if pool:
        for turn in range(turns):
            own_copy(turn).wait()

        def collect(j):
            n_copy(j, j).wait()
            for turn in range(turns):
                t_copy(j, j, turn).wait()

        others(collect)

        def taken(shape, dim):
            slot = lax.broadcasted_iota(jnp.int32, shape, dim)
            owner = slot // per
            r = slot % per
            held = jnp.zeros(shape, jnp.int32)
            for i in range(owners):
                held = jnp.where(owner == i, n_in[i][0:1, 0:1], held)
            b = (me - owner + owners) % owners + owners * (r // TILE)
            return home + TILE * b + r % TILE < held

        first = lax.broadcasted_iota(jnp.int32, (pool, pool), 0)
        second = lax.broadcasted_iota(jnp.int32, (pool, pool), 1)

        def ones(mask):
            return jnp.where(mask, 1.0, 0.0).astype(jnp.bfloat16)

        valid = taken((cap, pool), 1)
        spot = jnp.dot(ones(valid), ones(first < second), preferred_element_type=jnp.float32).astype(jnp.int32)
        sel[...] = ones(valid & (spot == lax.broadcasted_iota(jnp.int32, (cap, pool), 0)))
        valid = taken((pool, cap), 0)
        spot = jnp.dot(ones(second < first), ones(valid), preferred_element_type=jnp.float32).astype(jnp.int32)
        spread_sel[...] = ones(valid & (spot == lax.broadcasted_iota(jnp.int32, (pool, cap), 1)))
        picked[...] = jnp.dot(sel[...], pin[...], preferred_element_type=jnp.float32).astype(jnp.bfloat16)

        @pl.loop(0, 2 * (n - 1))
        def _(t):
            s, way, d = place(t)

            @pl.when(ahead(way, d))
            def _():
                part[d, pl.ds(home, cap)] = jnp.dot(picked[...], w[d], preferred_element_type=jnp.float32)

                @pl.when(first_hop(way))
                def _():
                    @pl.loop(0, pc)
                    def _(c):
                        send_first(way, s, d, hc + c)

        part[p, pl.ds(home, cap)] = jnp.dot(picked[...], w[p], preferred_element_type=jnp.float32)

    last_home(0, hc // 2)
    split = jnp.where(edge, early, done)
    if pool:
        pass_range(early, split)

    others(lambda j: a_copy(j, j).wait())

    width = owners * rank
    named = peer_ref[...]
    mine = lax.broadcasted_iota(jnp.int32, (width, rows), 0) // rank == named
    every = lax.dot_general(a_in[...].reshape(width, a_in.shape[2]), tok[...],
                            (((1,), (1,)), ((), ())), preferred_element_type=jnp.float32)
    kept = jnp.where(mine, every, 0.0).reshape(owners, rank, rows)
    total = kept[0]
    for j in range(1, owners):
        total = total + kept[j]
    s_out[...] = total

    @pl.loop(1, n)
    def _(k):
        q = lax.rem(p + k, n)
        s_copy(q, p).start()

    last_home(hc // 2, hc)

    if pool:
        pass_range(split, done)
        full = part[p, pl.ds(home, cap)]
        top = jnp.maximum(jnp.max(jnp.abs(full), axis=0, keepdims=True), LEAST)
        code = jnp.round(full * (STEPS / top))
        upper = jnp.floor(code * (1.0 / 256.0))
        lower = code - 256.0 * upper
        wide = (256.0 * jnp.dot(spread_sel[...], upper.astype(jnp.bfloat16), preferred_element_type=jnp.float32)
                + jnp.dot(spread_sel[...], lower.astype(jnp.bfloat16), preferred_element_type=jnp.float32))
        v_out[...] = top * (1.0 / STEPS)
        r_out[...] = wide.reshape(owners, per, blk).astype(jnp.int32).astype(LINK)

        def give(j):
            v_copy(j, me).start()
            r_copy(j, me).start()

        others(give)
        v_in[me] = v_out[...]
        r_in[me] = r_out[me]

    others(lambda j: b_copy(j, j).wait())

    @pl.loop(1, n)
    def _(k):
        q = lax.rem(p + k, n)
        s_copy(q, q).wait()
    total = s_out[...]
    for k in range(1, n):
        total = total + s_in[lax.rem(p + k, n)]
    spread = jnp.broadcast_to(total[None], (owners, rank, rows)).reshape(width, rows)
    shrink = jnp.where(mine, spread, 0.0).T
    high = shrink.astype(jnp.bfloat16)
    low = (shrink - high.astype(jnp.float32)).astype(jnp.bfloat16)
    ups = b_in[...].reshape(width, blk)
    out_ref[...] = (jnp.dot(high, ups, preferred_element_type=jnp.float32)
                    + jnp.dot(low, ups, preferred_element_type=jnp.float32))

    pass_range(done if pool else early, count + late)

    def finish(low, size, value):
        span = pl.ds(low, size)
        inside = low + lax.broadcasted_iota(jnp.int32, (size, blk), 0) < live[0]
        out_ref[span] = jnp.where(inside, out_ref[span] + value, 0.0)

    finish(0, home, part[p, pl.ds(0, home)])
    if pool:
        def gather(j):
            v_copy(j, j).wait()
            r_copy(j, j).wait()

        others(gather)

        @pl.loop(0, owners)
        def _(k):
            j = lax.rem(me + k, owners)
            value = decode(r_in[j], v_in[j])
            for turn in range(turns):
                b = k + owners * turn
                finish(pl.multiple_of(home + TILE * b, TILE), TILE, value[turn * TILE:(turn + 1) * TILE])

    @pl.loop(0, 2 * (n - 1))
    def _(t):
        s, way, d = place(t)

        @pl.when(ahead(way, d))
        def _():
            @pl.loop(0, ch)
            def _(c):
                q = jnp.where(way == 0, p + 1, p - 1)
                u_copy(way, s, c, q).wait_send()
                z_copy(way, s, c, q).wait_send()


def local(n, owners, tokens, w_kv, a_store, b_store, row_peer, wanted, live_rows):
    rows, feat = tokens.shape
    blk = w_kv.shape[1] // n
    held, rank = a_store.shape[:2]
    home, cap, rc = plan(owners, rows)
    ch = (home + cap) // rc
    pool = max(rows - home, owners * TILE)
    spare = max(cap, TILE)
    per = pool // owners
    turns = per // TILE
    vmem, dma = pltpu.VMEM, pltpu.SemaphoreType.DMA
    anyspec = pl.BlockSpec(memory_space=pl.ANY)
    return pl.pallas_call(
        functools.partial(kernel, n, owners, home, cap),
        out_shape=jax.ShapeDtypeStruct((rows, blk), jnp.float32),
        in_specs=[pl.BlockSpec(memory_space=pltpu.SMEM), pl.BlockSpec(memory_space=pltpu.SMEM), anyspec, anyspec, anyspec, anyspec,
                  pl.BlockSpec(memory_space=pltpu.VMEM)],
        out_specs=pl.BlockSpec(memory_space=pltpu.VMEM),
        scratch_shapes=[
            vmem((rows, feat), jnp.bfloat16),
            vmem((n, feat, blk), jnp.bfloat16),
            vmem((held, rank, feat), jnp.bfloat16),
            vmem((held, rank, blk), jnp.bfloat16),
            vmem((n, home + cap, blk), jnp.float32),
            vmem((2, n - 1, ch, rc, blk), LINK),
            vmem((2, n - 1, ch, rc, blk), LINK),
            vmem((2, n - 1, ch, 1, blk), jnp.float32),
            vmem((2, n - 1, ch, 1, blk), jnp.float32),
            vmem((owners, rank, feat), jnp.bfloat16),
            vmem((owners, rank, feat), jnp.bfloat16),
            vmem((owners, rank, blk), jnp.bfloat16),
            vmem((owners, rank, blk), jnp.bfloat16),
            vmem((rank, rows), jnp.float32),
            vmem((n, rank, rows), jnp.float32),
            vmem((pool, feat), jnp.bfloat16),
            vmem((spare, feat), jnp.bfloat16),
            vmem((spare, pool), jnp.bfloat16),
            vmem((pool, spare), jnp.bfloat16),
            vmem((TILE, 128), jnp.int32),
            vmem((owners, TILE, 128), jnp.int32),
            vmem((owners, per, blk), LINK),
            vmem((owners, per, blk), LINK),
            vmem((1, blk), jnp.float32),
            vmem((owners, 1, blk), jnp.float32),
            dma, dma((n,)), dma, dma,
            dma((2, n - 1, ch)), dma((2, n - 1, ch)),
            dma((2, n - 1, ch)), dma((2, n - 1, ch)),
            dma((owners,)), dma((owners,)), dma((owners,)), dma((owners,)),
            dma((n,)), dma((n,)),
            dma((owners, turns)), dma((owners, turns)), dma((turns,)),
            dma((owners,)), dma((owners,)), dma((owners,)), dma((owners,)), dma((owners,)), dma((owners,)),
        ],
        compiler_params=pltpu.CompilerParams(collective_id=0, has_side_effects=True),
        name="project",
    )(wanted, live_rows, tokens, w_kv, a_store, b_store, row_peer.reshape(1, rows))


def solution(mesh):
    in_specs = (
        P("dp", "tensor"),
        P("tensor", None),
        P("dp", None, "tensor"),
        P("dp", None, "tensor"),
        P("dp", None),
        P(),
        P("dp"),
    )
    body = functools.partial(local, mesh.shape["tensor"], mesh.shape["dp"])
    return jax.shard_map(body, mesh=mesh, in_specs=in_specs, out_specs=P("dp", "tensor"),
                         check_vma=False)
```
